32 devices in a mesh: depth: 4 (over y, x), surf: 8 (over z, core).
Axes of the slice: x: 2, y: 2, z: 4, core: 2. Of those that a mesh axis runs over, the one named last changes fastest.
Arguments:
- initial_warmth: float32 [256, 32, 2048], P('depth', 'surf'), may hold values from -6 to 6
- substance_label: int32 [256], replicated, may hold values from 0 to 3, never falling along the last dimension, each value on 1 to 128 neighbouring positions
- neighbour_kernel: float32 [4, 24], replicated, may hold values from 0.004 to 0.04
- arriving_heat_rate: float32 [32, 2048], P('surf'), may hold values from -3 to 3
- implicit_inverse_operator: float32 [256, 256], replicated, may hold values from 0 to 0.61, as said below
Outputs:
- final_temperature: float32 [256, 32, 2048], P('depth', 'surf')
The draws below stay inside these ranges and needn't reach their ends.
Inputs may be any that keep to these rules, and one draw needn't show every extreme that they name: `substance_label`: material numbers never fall from layer 0 (the heated side) to the last layer; every material holds at least one layer. `implicit_inverse_operator`: all entries are positive.
All inputs are finite; a program needn't handle non-finite values.
Results may differ from the reference program's by a relative error of at most 0.0001.
Values sent between devices are 32-bit elements; how exact they have to be, the bound alone decides.
A program may use at most 64 MiB of HBM per device.

```python
import math
import jax
import jax.numpy as jnp
import numpy as np
from jax import lax

L = 256
SY = 2048
STEPS = 3
NX = 32


def draw_initial_warmth(key, part):
    return jnp.clip(jax.random.normal(key, (L, NX, SY), jnp.float32), -6.0, 6.0)


def draw_implicit_inverse_operator(key, part):
    key_rough = jax.random.fold_in(key, 11)
    key_diag = jax.random.fold_in(key, 23)
    rows = jnp.arange(L)[:, None]
    cols = jnp.arange(L)[None, :]
    distance = jnp.abs(rows - cols).astype(jnp.float32)
    length_total = L / 8.0
    ratio = jnp.exp(-1.0 / length_total)
    rough = jax.random.uniform(key_rough, (L, L), jnp.float32, 0.5, 1.5)
    diag_gain = jax.random.uniform(key_diag, (L,), jnp.float32, 0.9, 1.1)
    off_part = 0.3 * rough * jnp.exp(-distance / length_total) * (1.0 - ratio) / (2.0 * ratio)
    diagonal_portion = jnp.broadcast_to(0.55 * diag_gain[:, None], (L, L))
    return jnp.where(distance == 0.0, diagonal_portion, off_part)


def block_scale(own_key, extent, shards, least, top_value):
    def one(axis_at, blocks):
        draws = jax.random.uniform(jax.random.fold_in(jax.random.fold_in(own_key, 6), axis_at), (blocks,), jnp.float32, least / len(shards), top_value / len(shards))
        return jnp.repeat(jnp.exp(draws), extent[axis_at] // blocks).reshape((-1,) + (1,) * (len(extent) - axis_at - 1))

    gain = one(*shards[0])
    for cut in shards[1:]:
        gain = gain * one(*cut)
    return gain


def length_profile(count, total, limit, lean):
    portions = [(1 << 20) // math.isqrt(grade ** lean) + 1 for grade in range(2, count + 1)]
    spare, holding = total - limit - (count - 1), [1] * (count - 1)
    while spare > 0:
        free = [i for i in range(count - 1) if holding[i] < limit]
        mass, remaining = sum([portions[i] for i in free]), spare
        for i in free:
            addition = min(limit - holding[i], max(1, remaining * portions[i] // mass), spare)
            holding[i] = holding[i] + addition
            spare = spare - addition
    return np.array([limit] + holding)


def uneven_parts(rng, count, total, most, skew):
    if count == 2:
        one = jax.random.randint(rng, (), max(1, total - most), min(most, total - 1) + 1)
        return jnp.stack([one, total - one])
    tallies = jnp.asarray(length_profile(count, total, most, skew), jnp.int32)
    couples = (count - 1) // 2
    source_of, sink = tallies[1:1 + 2 * couples:2], tallies[2:2 + 2 * couples:2]
    margin = jnp.minimum(source_of - 1, most - sink)
    passed = jax.random.randint(jax.random.fold_in(rng, 1), (couples,), 0, 1 << 20) % (margin + 1)
    tallies = tallies.at[1:1 + 2 * couples:2].set(source_of - passed).at[2:2 + 2 * couples:2].set(sink + passed)
    return tallies[jax.random.permutation(jax.random.fold_in(rng, 2), count)]


def gaussian(rng, dims, width, bound, cuts=(), kind=jnp.bfloat16):
    entries = jax.random.normal(rng, dims, jnp.float32) * width
    if len(cuts) > 0:
        entries = block_scale(rng, dims, cuts, -0.22, 0.18) * entries
    return jnp.clip(entries, min=-bound, max=bound).astype(kind)


def setup_inputs(seed: int = 0) -> dict:
    splits = jax.random.split(jax.random.key(seed), 6)
    return {
        "initial_warmth": draw_initial_warmth(jax.random.fold_in(splits[5], 71), 0),
        "substance_label": jnp.searchsorted(jnp.cumsum(uneven_parts(splits[1], 4, L, L // 2, 0)), jnp.arange(L), side="right").astype(jnp.int32),
        "neighbour_kernel": jnp.clip(jnp.exp(jax.random.uniform(splits[2], (4, 24), jnp.float32, math.log(0.004), math.log(0.04))), 0.004, 0.04),
        "arriving_heat_rate": gaussian(splits[3], (NX, SY), 0.5, 3.0, ((0, 8),), jnp.float32),
        "implicit_inverse_operator": draw_implicit_inverse_operator(jax.random.fold_in(splits[5], 71), 0),
    }


neighbours = [(row_step, column_stride) for row_step in range(-2, 3) for column_stride in range(-2, 3) if row_step != 0 or column_stride != 0]


def coefficients(substance_label, neighbour_kernel):
    chosen = (substance_label[:, None] == jnp.arange(4, dtype=jnp.int32)[None, :]).astype(neighbour_kernel.dtype)
    return jnp.sum(chosen[:, :, None] * neighbour_kernel[None, :, :], axis=1)


def sheet_diffusion(operands):
    plane, kernel_factors = operands
    bordered_field = jnp.pad(plane, 2)
    tally_lines, grid_breadth = plane.shape
    accumulated = jnp.zeros_like(plane)
    for place_index, offset in enumerate(neighbours):
        displaced_field = bordered_field[2 + offset[0]:2 + offset[0] + tally_lines, 2 + offset[1]:2 + offset[1] + grid_breadth]
        accumulated = accumulated + kernel_factors[place_index] * (displaced_field - plane)
    return plane + accumulated


def reference(initial_warmth, substance_label, neighbour_kernel, arriving_heat_rate, implicit_inverse_operator):
    sheet_factors = coefficients(substance_label, neighbour_kernel)
    current_thermal_state = initial_warmth
    for step_index in range(STEPS):
        advance_explicit_step = lax.map(sheet_diffusion, (current_thermal_state, sheet_factors))
        advance_explicit_step = advance_explicit_step.at[0].add(arriving_heat_rate)
        current_thermal_state = jnp.einsum("mq,qhl->mhl", implicit_inverse_operator, advance_explicit_step, precision=lax.Precision.HIGHEST)
    return current_thermal_state
```

```python
import functools

import jax
import jax.numpy as jnp
from jax import lax
from jax.experimental import pallas as pl
from jax.experimental.pallas import tpu as pltpu
from jax.sharding import PartitionSpec as P

LANES = 128
STRIP = 6
PAD = 16
SPAN = LANES + 2 * PAD
WIDE = LANES + 16
MESH = pl.DeviceIdType.MESH
NT = (((1,), (1,)), ((), ()))


def flipped(rank, mask, count):
    out, bit = 0, 1
    while bit < count:
        mine = (rank // bit) % 2
        out = out + bit * ((1 - mine) if (mask // bit) % 2 else mine)
        bit *= 2
    return out


def kernel(
    nd, ns, tiles,
    x_ref, lab_ref, nk_ref, heat_ref, op_ref, out_ref,
    xr, raw, eb, eraw, et, s0, s1, s2, hot, ex, ob, coef, op3, opt,
    l_sem, a_send, a_recv, a_loc, z_send, z_recv, o_send, o_recv, o_loc,
):
    d = lax.axis_index("depth")
    s = lax.axis_index("surf")
    layers_here, rows, width = x_ref.shape
    layers = op_ref.shape[0]
    halves = layers // LANES
    cols = tiles * LANES
    states = (s0, s1, s2)
    peers = [j for j in range(nd - 1, 0, -1)]
    has = (s > 0, s < ns - 1)
    near = (s - 1, s + 1)
    mine = pl.ds(pl.multiple_of(d * layers_here, 8), layers_here)

    def block_cols(b, t):
        return pl.ds(pl.multiple_of(b * cols + t * LANES, LANES), LANES)

    def load(r):
        return pltpu.make_async_copy(x_ref.at[:, r, :], xr.at[r], l_sem.at[r])

    def spread(j, t):
        p = flipped(d, j, nd)
        if t == tiles:
            src, dst = eb.at[p], eraw.at[mine]
        else:
            src, dst = xr.at[:, :, block_cols(p, t)], raw.at[t, :, mine]
        return pltpu.make_async_remote_copy(
            src, dst, a_send.at[j, t], a_recv.at[j, t],
            device_id={"depth": p}, device_id_type=MESH,
        )

    def keep(t):
        if t == tiles:
            src, dst = eb.at[d], eraw.at[mine]
        else:
            src, dst = xr.at[:, :, block_cols(d, t)], raw.at[t, :, mine]
        return pltpu.make_async_copy(src, dst, a_loc.at[t])

    def trade(n, t, side):
        part = pl.ds(PAD - STRIP + 2 * n, LANES + 2 * STRIP - 4 * n)
        return pltpu.make_async_remote_copy(
            states[n].at[t, :, pl.ds(2 + 2 * side, 2), part],
            states[n].at[t, :, pl.ds(6 - 6 * side, 2), part],
            z_send.at[n, t, side], z_recv.at[n, t, side],
            device_id={"surf": near[side]}, device_id_type=MESH,
        )

    def give_back(j, t, r):
        p = flipped(d, j, nd)
        theirs = pl.ds(pl.multiple_of(p * layers_here, 8), layers_here)
        return pltpu.make_async_remote_copy(
            ob.at[t, r, theirs], out_ref.at[:, r, block_cols(d, t)],
            o_send.at[j, t, r], o_recv.at[j, t, r],
            device_id={"depth": p}, device_id_type=MESH,
        )

    def put_home(t, r):
        return pltpu.make_async_copy(
            ob.at[t, r, mine], out_ref.at[:, r, block_cols(d, t)], o_loc.at[t, r]
        )

    for r in range(rows):
        load(r).start()

    barrier = pltpu.get_barrier_semaphore()
    for j in peers:
        pl.semaphore_signal(
            barrier, inc=1, device_id={"depth": flipped(d, j, nd)}, device_id_type=MESH
        )
    for side in range(2):
        @pl.when(has[side])
        def _():
            pl.semaphore_signal(
                barrier, inc=1, device_id={"surf": near[side]}, device_id_type=MESH
            )
    at_end = jnp.where(s > 0, 0, 1) + jnp.where(s < ns - 1, 0, 1)
    for r in range(rows):
        load(r).wait()
    pl.semaphore_wait(barrier, nd + 1 - at_end)

    for j in peers:
        spread(j, 0).start()

    lane8 = lax.broadcasted_iota(jnp.int32, (8, LANES), 1)
    group = LANES // rows
    for b in range(nd):
        @pl.loop(0, layers_here // 8)
        def _(g):
            part = pl.ds(pl.multiple_of(g * 8, 8), 8)
            packed = jnp.zeros((8, LANES), jnp.float32)
            for r in range(rows):
                edge = jnp.zeros((8, LANES), jnp.float32)
                for i in range(tiles):
                    at = b * cols + (i + 1) * LANES
                    if at < width:
                        v = xr[r, part, at:at + LANES]
                        v = jnp.where(lane8 < STRIP, v, 0.0)
                        shift = STRIP * i + group * r
                        edge = edge + (pltpu.roll(v, shift, 1) if shift else v)
                if b > 0:
                    v = xr[r, part, b * cols - LANES:b * cols]
                    v = jnp.where(lane8 >= LANES - STRIP, v, 0.0)
                    shift = (group * (r + 1)) % LANES
                    edge = edge + (pltpu.roll(v, shift, 1) if shift else v)
                packed = packed + edge
            eb[b, part, :] = packed
    for t in [tiles] + list(range(1, tiles)):
        for j in peers:
            spread(j, t).start()
    for t in range(tiles + 1):
        keep(t).start()

    for h in range(halves):
        kind = jnp.broadcast_to(lab_ref[:, h * LANES:(h + 1) * LANES], (8, LANES))
        total = jnp.zeros((8, LANES), jnp.float32)
        for k in range(24):
            c = jnp.where(
                kind == 0, nk_ref[0, k],
                jnp.where(kind == 1, nk_ref[1, k], jnp.where(kind == 2, nk_ref[2, k], nk_ref[3, k])),
            )
            coef[h, k if k < 12 else k + 1] = c
            total = total + c
        coef[h, 12] = 1.0 - total

    high = op_ref[...].astype(jnp.bfloat16)
    low = (op_ref[...] - high.astype(jnp.float32)).astype(jnp.bfloat16)
    op3[:, 0:layers] = high
    op3[:, layers:2 * layers] = high
    op3[:, 2 * layers:] = low
    turned = jnp.transpose(op_ref[...])
    high = turned.astype(jnp.bfloat16)
    low = (turned - high.astype(jnp.float32)).astype(jnp.bfloat16)
    opt[0:layers, :] = high
    opt[layers:2 * layers, :] = high
    opt[2 * layers:, :] = low

    top = lax.broadcasted_iota(jnp.int32, (LANES, LANES), 0) == 0
    for t in range(-1, tiles + 1):
        b = d if 0 <= t < tiles else (lax.rem(d + nd - 1, nd) if t < 0 else lax.rem(d + 1, nd))
        for r in range(rows):
            line = heat_ref[r:r + 1, block_cols(b, t % tiles)]
            tall = jnp.transpose(jnp.where(top, jnp.broadcast_to(line, (LANES, LANES)), 0.0))
            hot[r, (t + 1) * LANES:(t + 2) * LANES, :] = tall

    for side in range(2):
        @pl.when(jnp.logical_not(has[side]))
        def _():
            @pl.loop(0, tiles)
            def _(t):
                for state in states:
                    for h in range(halves):
                        for r in range(2):
                            state[t, h, 6 * side + r] = jnp.zeros((SPAN, LANES), jnp.float32)

    def lateral(src, t, first, groups):
        for h in range(halves):
            cs = [coef[h, k] for k in range(25)]

            @pl.loop(0, groups // 2)
            def _(g):
                at = pl.multiple_of(first + g * 16, 8)
                whole = [[], [], [], []]
                for u in range(2):
                    acc = [None] * rows
                    for i in range(rows + 4):
                        for q in range(5):
                            view = src[t, h, i, pl.ds(at + 8 * u + q - 2, 8), :]
                            for r in range(max(0, i - 4), min(rows, i + 1)):
                                term = cs[(i - r) * 5 + q] * view
                                acc[r] = term if acc[r] is None else acc[r] + term
                    for r in range(rows):
                        v = acc[r]
                        if h == 0:
                            v = v + hot[r, pl.ds(at + 8 * u + (t + 1) * LANES - PAD, 8), :]
                        whole[r].append(v)
                for r in range(rows):
                    v = jnp.concatenate(whole[r], axis=0)
                    eh = v.astype(jnp.bfloat16)
                    el = (v - eh.astype(jnp.float32)).astype(jnp.bfloat16)
                    here = pl.ds(pl.multiple_of(g * 16, 16), 16)
                    ex[r, here, h * LANES:(h + 1) * LANES] = eh
                    ex[r, here, layers + h * LANES:layers + (h + 1) * LANES] = el

    def implicit(t, dst):
        for r in range(rows):
            e = ex[r]
            y = jnp.dot(
                jnp.concatenate([e, e[:, :layers]], axis=1), opt[...],
                preferred_element_type=jnp.float32,
            )
            for h in range(halves):
                dst[t, h, 2 + r, PAD - 8:PAD - 8 + WIDE, :] = y[:, h * LANES:(h + 1) * LANES]
        if t == 0:
            @pl.when(d == 0)
            def _():
                for h in range(halves):
                    for r in range(rows):
                        dst[t, h, 2 + r, PAD - 8:PAD, :] = jnp.zeros((8, LANES), jnp.float32)
        if t == tiles - 1:
            @pl.when(d == nd - 1)
            def _():
                for h in range(halves):
                    for r in range(rows):
                        dst[t, h, 2 + r, PAD + LANES:PAD + LANES + 8, :] = jnp.zeros((8, LANES), jnp.float32)

    def trades(n, t):
        for side in range(2):
            @pl.when(has[side])
            def _():
                trade(n, t, side).start()

    def halo(n, t):
        for side in range(2):
            @pl.when(has[side])
            def _():
                trade(n, t, 1 - side).wait_recv()

    def arrive(t):
        if t == 0:
            for j in peers:
                spread(j, tiles).wait_recv()
            keep(tiles).wait()
            for h in range(halves):
                et[h] = jnp.transpose(eraw[h * LANES:(h + 1) * LANES, :])
        for j in peers:
            spread(j, t).wait_recv()
        keep(t).wait()
        for h in range(halves):
            for r in range(rows):
                s0[t, h, 2 + r, PAD:PAD + LANES, :] = jnp.transpose(
                    raw[t, r, h * LANES:(h + 1) * LANES, :]
                )
                if t == 0:
                    left = et[h, group * (r + 1) - 8:group * (r + 1), :]
                else:
                    left = s0[t - 1, h, 2 + r, PAD + LANES - 8:PAD + LANES, :]
                s0[t, h, 2 + r, PAD - 8:PAD, :] = left
                at = group * r + STRIP * t
                s0[t, h, 2 + r, PAD + LANES:PAD + LANES + 8, :] = et[h, at:at + 8, :]
        trades(0, t)

    def step(n, t):
        halo(n - 1, t)
        lateral(states[n - 1], t, PAD - 8, WIDE // 8)
        implicit(t, states[n])
        trades(n, t)

    def last(t):
        halo(2, t)
        lateral(s2, t, PAD, LANES // 8)
        for pair in range(rows // 2):
            e = jnp.concatenate([ex[2 * pair, 0:LANES], ex[2 * pair + 1, 0:LANES]], axis=0)
            y = lax.dot_general(
                op3[...], jnp.concatenate([e, e[:, :layers]], axis=1), NT,
                preferred_element_type=jnp.float32,
            )
            ob[t, 2 * pair] = y[:, :LANES]
            ob[t, 2 * pair + 1] = y[:, LANES:]
        for j in peers:
            for r in range(rows):
                give_back(j, t, r).start()
        for r in range(rows):
            put_home(t, r).start()

    for stage in range(tiles + 3):
        if stage < tiles:
            arrive(stage)
        if 0 <= stage - 1 < tiles:
            step(1, stage - 1)
        if 0 <= stage - 2 < tiles:
            step(2, stage - 2)
        if 0 <= stage - 3 < tiles:
            last(stage - 3)

    for t in range(tiles):
        for r in range(rows):
            for j in peers:
                give_back(j, t, r).wait()
            put_home(t, r).wait()
    for t in range(tiles + 1):
        for j in peers:
            spread(j, t).wait_send()
    for t in range(tiles):
        for n in range(3):
            for side in range(2):
                @pl.when(has[side])
                def _():
                    trade(n, t, side).wait_send()


def shards(
    nd, ns,
    initial_warmth, substance_label, neighbour_kernel, arriving_heat_rate, implicit_inverse_operator,
):
    layers_here, rows, width = initial_warmth.shape
    layers = implicit_inverse_operator.shape[0]
    tiles = width // nd // LANES
    halves = layers // LANES
    labels = substance_label[None, :]
    f32, dma = jnp.float32, pltpu.SemaphoreType.DMA
    vmem = pl.BlockSpec(memory_space=pltpu.VMEM)
    state = pltpu.VMEM((tiles, halves, rows + 4, SPAN, LANES), f32)
    return pl.pallas_call(
        functools.partial(kernel, nd, ns, tiles),
        out_shape=jax.ShapeDtypeStruct(initial_warmth.shape, f32),
        in_specs=[
            pl.BlockSpec(memory_space=pl.ANY), vmem, pl.BlockSpec(memory_space=pltpu.SMEM), vmem, vmem,
        ],
        out_specs=pl.BlockSpec(memory_space=pl.ANY),
        scratch_shapes=[
            pltpu.VMEM((rows, layers_here, width), f32),
            pltpu.VMEM((tiles, rows, layers, LANES), f32),
            pltpu.VMEM((nd, layers_here, LANES), f32),
            pltpu.VMEM((layers, LANES), f32),
            pltpu.VMEM((halves, LANES, LANES), f32),
            state, state, state,
            pltpu.VMEM((rows, (tiles + 2) * LANES, LANES), f32),
            pltpu.VMEM((rows, WIDE, 2 * layers), jnp.bfloat16),
            pltpu.VMEM((tiles, rows, layers, LANES), f32),
            pltpu.VMEM((halves, 25, 8, LANES), f32),
            pltpu.VMEM((layers, 3 * layers), jnp.bfloat16),
            pltpu.VMEM((3 * layers, layers), jnp.bfloat16),
            dma((rows,)),
            dma((nd, tiles + 1)), dma((nd, tiles + 1)), dma((tiles + 1,)),
            dma((3, tiles, 2)), dma((3, tiles, 2)),
            dma((nd, tiles, rows)), dma((nd, tiles, rows)), dma((tiles, rows)),
        ],
        compiler_params=pltpu.CompilerParams(
            collective_id=0, has_side_effects=True, vmem_limit_bytes=60 * 1024 * 1024
        ),
    )(initial_warmth, labels, neighbour_kernel, arriving_heat_rate, implicit_inverse_operator)


def solution(mesh):
    return jax.shard_map(
        functools.partial(shards, mesh.shape["depth"], mesh.shape["surf"]),
        mesh=mesh,
        in_specs=(P("depth", "surf", None), P(), P(), P("surf", None), P()),
        out_specs=P("depth", "surf", None),
        check_vma=False,
    )
```

```python
import functools

import jax
import jax.numpy as jnp
from jax import lax
from jax.experimental import pallas as pl
from jax.experimental.pallas import tpu as pltpu
from jax.sharding import PartitionSpec as P

LANES = 128
STRIP = 6
PAD = 16
SPAN = LANES + 2 * PAD
WIDE = LANES + 16
MESH = pl.DeviceIdType.MESH
NT = (((1,), (1,)), ((), ()))


def flipped(rank, mask, count):
    out, bit = 0, 1
    while bit < count:
        mine = (rank // bit) % 2
        out = out + bit * ((1 - mine) if (mask // bit) % 2 else mine)
        bit *= 2
    return out


def kernel(
    nd, ns, tiles,
    x_ref, lab_hbm, nk_hbm, heat_hbm, op_hbm, out_ref,
    lab_ref, nk_ref, heat_ref, op_ref,
    xr, raw, side_raw, eb, eraw, et, side_et, hb, s0, s1, s2, hot, ex, ob, coef, op3, opt,
    i_sem, l_sem, a_send, a_recv, a_loc, f_send, f_recv, e_send, e_recv, h_send, h_recv,
    z_send, z_recv, o_send, o_recv, o_loc,
):
    d = lax.axis_index("depth")
    s = lax.axis_index("surf")
    layers_here, rows, width = x_ref.shape
    layers = op_ref.shape[0]
    halves = layers // LANES
    cols = tiles * LANES
    peers = [j for j in range(nd - 1, 0, -1)]
    has = (s > 0, s < ns - 1)
    near = (s - 1, s + 1)
    mine = pl.ds(pl.multiple_of(d * layers_here, 8), layers_here)

    def block_cols(b, t):
        return pl.ds(pl.multiple_of(b * cols + t * LANES, LANES), LANES)

    def fetch(k):
        src = (lab_hbm, nk_hbm, heat_hbm, op_hbm)[k]
        return pltpu.make_async_copy(src, (lab_ref, nk_ref, heat_ref, op_ref)[k], i_sem.at[k])

    def load(r):
        return pltpu.make_async_copy(x_ref.at[:, r, :], xr.at[r], l_sem.at[r])

    def spread(j, t):
        p = flipped(d, j, nd)
        if t == tiles:
            src, dst = eb.at[p], eraw.at[mine]
        else:
            src, dst = xr.at[:, :, block_cols(p, t)], raw.at[t, :, mine]
        return pltpu.make_async_remote_copy(
            src, dst, a_send.at[j, t], a_recv.at[j, t],
            device_id={"depth": p}, device_id_type=MESH,
        )

    def keep(t):
        if t == tiles:
            src, dst = eb.at[d], eraw.at[mine]
        else:
            src, dst = xr.at[:, :, block_cols(d, t)], raw.at[t, :, mine]
        return pltpu.make_async_copy(src, dst, a_loc.at[t])

    def forward(side, j, t):
        p = flipped(d, j, nd)
        part = pl.ds(pl.multiple_of(p * layers_here, 8), layers_here)
        src = raw.at[t, :, part] if j else xr.at[:, :, block_cols(d, t)]
        return pltpu.make_async_remote_copy(
            src, side_raw.at[t, 1 - side, :, part], f_send.at[side, j, t], f_recv.at[side, j, t],
            device_id={"surf": near[side]}, device_id_type=MESH,
        )

    def forward_strips(side):
        return pltpu.make_async_remote_copy(
            et, side_et.at[1 - side], e_send.at[side], e_recv.at[side],
            device_id={"surf": near[side]}, device_id_type=MESH,
        )

    def heat_out(side):
        return pltpu.make_async_remote_copy(
            heat_hbm, hb.at[1 - side], h_send.at[side], h_recv.at[side],
            device_id={"surf": near[side]}, device_id_type=MESH,
        )

    def trade(t, side, h):
        part = pl.ds(PAD - 2, LANES + 4)
        return pltpu.make_async_remote_copy(
            s2.at[t, h, pl.ds(2 + 2 * side, 2), part],
            s2.at[t, h, pl.ds(6 - 6 * side, 2), part],
            z_send.at[t, side, h], z_recv.at[t, side, h],
            device_id={"surf": near[side]}, device_id_type=MESH,
        )

    def at_sides(action):
        for side in range(2):
            @pl.when(has[side])
            def _():
                action(side)

    def give_back(j, t, r):
        p = flipped(d, j, nd)
        theirs = pl.ds(pl.multiple_of(p * layers_here, 8), layers_here)
        return pltpu.make_async_remote_copy(
            ob.at[t, r, theirs], out_ref.at[:, r, block_cols(d, t)],
            o_send.at[j, t, r], o_recv.at[j, t, r],
            device_id={"depth": p}, device_id_type=MESH,
        )

    def put_home(t, r):
        return pltpu.make_async_copy(
            ob.at[t, r, mine], out_ref.at[:, r, block_cols(d, t)], o_loc.at[t, r]
        )

    barrier = pltpu.get_barrier_semaphore()
    for j in peers:
        pl.semaphore_signal(
            barrier, inc=1, device_id={"depth": flipped(d, j, nd)}, device_id_type=MESH
        )
    for side in range(2):
        @pl.when(has[side])
        def _():
            pl.semaphore_signal(
                barrier, inc=1, device_id={"surf": near[side]}, device_id_type=MESH
            )
    at_end = jnp.where(s > 0, 0, 1) + jnp.where(s < ns - 1, 0, 1)
    for r in range(rows):
        load(r).start()
    for k in range(4):
        fetch(k).start()
    for r in range(rows):
        load(r).wait()
    pl.semaphore_wait(barrier, nd + 1 - at_end)

    own = 2
    spread(peers[0], 0).start()
    def first_sends(side):
        forward(side, 0, 0).start()
        heat_out(side).start()
        for t in range(1, min(own, tiles)):
            forward(side, 0, t).start()

    at_sides(first_sends)

    lane8 = lax.broadcasted_iota(jnp.int32, (8, LANES), 1)
    group = LANES // rows
    for b in range(nd):
        @pl.loop(0, layers_here // 8)
        def _(g):
            part = pl.ds(pl.multiple_of(g * 8, 8), 8)
            packed = jnp.zeros((8, LANES), jnp.float32)
            for r in range(rows):
                edge = jnp.zeros((8, LANES), jnp.float32)
                for i in range(tiles):
                    at = b * cols + (i + 1) * LANES
                    if at < width:
                        v = xr[r, part, at:at + LANES]
                        v = jnp.where(lane8 < STRIP, v, 0.0)
                        shift = STRIP * i + group * r
                        edge = edge + (pltpu.roll(v, shift, 1) if shift else v)
                if b > 0:
                    v = xr[r, part, b * cols - LANES:b * cols]
                    v = jnp.where(lane8 >= LANES - STRIP, v, 0.0)
                    shift = (group * (r + 1)) % LANES
                    edge = edge + (pltpu.roll(v, shift, 1) if shift else v)
                packed = packed + edge
            eb[b, part, :] = packed
    for j in peers:
        spread(j, tiles).start()
    for j in peers[1:]:
        spread(j, 0).start()
    for t in range(1, tiles):
        for j in peers:
            spread(j, t).start()
    for t in range(tiles + 1):
        keep(t).start()

    for k in range(4):
        fetch(k).wait()
    for h in range(halves):
        kind = jnp.broadcast_to(lab_ref[:, h * LANES:(h + 1) * LANES], (8, LANES))
        total = jnp.zeros((8, LANES), jnp.float32)
        for k in range(24):
            c = jnp.where(
                kind == 0, nk_ref[0, k],
                jnp.where(kind == 1, nk_ref[1, k], jnp.where(kind == 2, nk_ref[2, k], nk_ref[3, k])),
            )
            coef[h, k if k < 12 else k + 1] = c
            total = total + c
        coef[h, 12] = 1.0 - total

    high = op_ref[...].astype(jnp.bfloat16)
    low = (op_ref[...] - high.astype(jnp.float32)).astype(jnp.bfloat16)
    op3[:, 0:layers] = high
    op3[:, layers:2 * layers] = high
    op3[:, 2 * layers:] = low
    turned = jnp.transpose(op_ref[...])
    high = turned.astype(jnp.bfloat16)
    low = (turned - high.astype(jnp.float32)).astype(jnp.bfloat16)
    opt[0:layers, :] = high
    opt[layers:2 * layers, :] = high
    opt[2 * layers:, :] = low

    top = lax.broadcasted_iota(jnp.int32, (LANES, LANES), 0) == 0

    def heat_row(src, row, to):
        for t in range(-1, tiles + 1):
            b = d if 0 <= t < tiles else (lax.rem(d + nd - 1, nd) if t < 0 else lax.rem(d + 1, nd))
            line = src[row:row + 1, block_cols(b, t % tiles)]
            tall = jnp.transpose(jnp.where(top, jnp.broadcast_to(line, (LANES, LANES)), 0.0))
            hot[to, (t + 1) * LANES:(t + 2) * LANES, :] = tall

    for r in range(rows):
        heat_row(heat_ref, r, 2 + r)

    for side in range(2):
        @pl.when(jnp.logical_not(has[side]))
        def _():
            @pl.loop(0, tiles)
            def _(t):
                for h in range(halves):
                    for r in range(rows):
                        s0[t, h, 8 * side + r] = jnp.zeros((SPAN, LANES), jnp.float32)
                    for r in range(2):
                        s2[t, h, 6 * side + r] = jnp.zeros((SPAN, LANES), jnp.float32)

    def side_heat(side):
        heat_out(1 - side).wait_recv()
        for r in range(2):
            heat_row(hb.at[side], r + 2 - 2 * side, r + 6 * side)

    at_sides(side_heat)

    def lateral(src, t, first, groups, made, warm, ready=None):
        for h in range(halves):
            if ready is not None:
                ready(h)
            cs = [coef[h, k] for k in range(25)]

            @pl.loop(0, groups // 2)
            def _(g):
                at = pl.multiple_of(first + g * 16, 8)
                whole = [[] for _ in range(made)]
                for u in range(2):
                    acc = [None] * made
                    for i in range(made + 4):
                        for q in range(5):
                            view = src[t, h, i, pl.ds(at + 8 * u + q - 2, 8), :]
                            for r in range(max(0, i - 4), min(made, i + 1)):
                                term = cs[(i - r) * 5 + q] * view
                                acc[r] = term if acc[r] is None else acc[r] + term
                    for r in range(made):
                        v = acc[r]
                        if h == 0:
                            v = v + hot[warm + r, pl.ds(at + 8 * u + (t + 1) * LANES - PAD, 8), :]
                        whole[r].append(v)
                for r in range(made):
                    v = jnp.concatenate(whole[r], axis=0)
                    eh = v.astype(jnp.bfloat16)
                    el = (v - eh.astype(jnp.float32)).astype(jnp.bfloat16)
                    here = pl.ds(pl.multiple_of(g * 16, 16), 16)
                    ex[r, here, h * LANES:(h + 1) * LANES] = eh
                    ex[r, here, layers + h * LANES:layers + (h + 1) * LANES] = el

    def implicit(t, dst, made, to):
        for r in range(made):
            e = ex[r]
            y = jnp.dot(
                jnp.concatenate([e, e[:, :layers]], axis=1), opt[...],
                preferred_element_type=jnp.float32,
            )
            for h in range(halves):
                dst[t, h, to + r, PAD - 8:PAD - 8 + WIDE, :] = y[:, h * LANES:(h + 1) * LANES]
        for at, edge in ((PAD - 8, jnp.logical_and(t == 0, d == 0)),
                         (PAD + LANES, jnp.logical_and(t == tiles - 1, d == nd - 1))):
            if t not in (0, tiles - 1):
                continue

            @pl.when(edge)
            def _():
                for h in range(halves):
                    for r in range(made):
                        dst[t, h, to + r, at:at + 8, :] = jnp.zeros((8, LANES), jnp.float32)

    def receive(t, k):
        for j in (peers[k:k + 1] if k < 2 else peers[2:]):
            spread(j, t).wait_recv()
            at_sides(lambda side: forward(side, j, t).start())
        if t == 0 and k == 0:
            for j in peers:
                spread(j, tiles).wait_recv()
            keep(tiles).wait()
            for h in range(halves):
                et[h] = jnp.transpose(eraw[h * LANES:(h + 1) * LANES, :])
            at_sides(lambda side: forward_strips(side).start())
        if k == 2 and t + own < tiles:
            at_sides(lambda side: forward(side, 0, t + own).start())

    def unpack(t, src, strips, row, to):
        for h in range(halves):
            s0[t, h, to, PAD:PAD + LANES, :] = jnp.transpose(
                src[row, h * LANES:(h + 1) * LANES, :]
            )
            if t == 0:
                left = strips[h, group * (row + 1) - 8:group * (row + 1), :]
            else:
                left = s0[t - 1, h, to, PAD + LANES - 8:PAD + LANES, :]
            s0[t, h, to, PAD - 8:PAD, :] = left
            at = group * row + STRIP * t
            s0[t, h, to, PAD + LANES:PAD + LANES + 8, :] = strips[h, at:at + 8, :]

    def arrange(t):
        keep(t).wait()
        for r in range(rows):
            unpack(t, raw.at[t], et, r, rows + r)

    def arrange_side(t):
        def one(side):
            if t == 0:
                forward_strips(1 - side).wait_recv()
            for j in range(nd):
                forward(1 - side, j, t).wait_recv()
            for r in range(rows):
                unpack(t, side_raw.at[t, side], side_et.at[side], r, 2 * rows * side + r)

        at_sides(one)

    def step1(t):
        lateral(s0, t, PAD - 8, WIDE // 8, rows + 4, 0)
        implicit(t, s1, rows + 4, 0)
        for side in range(2):
            @pl.when(jnp.logical_not(has[side]))
            def _():
                for h in range(halves):
                    for r in range(2):
                        s1[t, h, 6 * side + r] = jnp.zeros((SPAN, LANES), jnp.float32)

    def step2(t):
        lateral(s1, t, PAD - 8, WIDE // 8, rows, 2)
        implicit(t, s2, rows, 2)
        for h in range(halves):
            at_sides(lambda side: trade(t, side, h).start())

    def last(t):
        def ready(h):
            at_sides(lambda side: trade(t, 1 - side, h).wait_recv())

        lateral(s2, t, PAD, LANES // 8, rows, 2, ready)
        for pair in range(rows // 2):
            e = jnp.concatenate([ex[2 * pair, 0:LANES], ex[2 * pair + 1, 0:LANES]], axis=0)
            y = lax.dot_general(
                op3[...], jnp.concatenate([e, e[:, :layers]], axis=1), NT,
                preferred_element_type=jnp.float32,
            )
            for r in range(2 * pair, 2 * pair + 2):
                ob[t, r] = y[:, (r % 2) * LANES:(r % 2 + 1) * LANES]
                for j in peers:
                    give_back(j, t, r).start()
                put_home(t, r).start()

    plan = (
        "P0", "Q0", "R0", "P1", "Q1", "a0", "h0", "R1", "10", "a1", "P2",
        "20", "h1", "11", "Q2", "R2", "21", "P3", "Q3", "30", "a2", "h2",
        "R3", "12", "31", "a3", "22", "h3", "13", "23", "32", "33",
    )
    for item in plan:
        t = int(item[1])
        if t < tiles:
            {
                "P": lambda: receive(t, 0), "Q": lambda: receive(t, 1), "R": lambda: receive(t, 2),
                "a": lambda: arrange(t), "h": lambda: arrange_side(t),
                "1": lambda: step1(t), "2": lambda: step2(t), "3": lambda: last(t),
            }[item[0]]()

    for t in range(tiles):
        for r in range(rows):
            for j in peers:
                give_back(j, t, r).wait()
            put_home(t, r).wait()
    for t in range(tiles + 1):
        for j in peers:
            spread(j, t).wait_send()
    def sent(side):
        forward_strips(side).wait_send()
        heat_out(side).wait_send()
        for t in range(tiles):
            for j in range(nd):
                forward(side, j, t).wait_send()
            for h in range(halves):
                trade(t, side, h).wait_send()

    at_sides(sent)


def shards(
    nd, ns,
    initial_warmth, substance_label, neighbour_kernel, arriving_heat_rate, implicit_inverse_operator,
):
    layers_here, rows, width = initial_warmth.shape
    layers = implicit_inverse_operator.shape[0]
    tiles = width // nd // LANES
    halves = layers // LANES
    labels = substance_label[None, :]
    f32, dma = jnp.float32, pltpu.SemaphoreType.DMA

    def state(high):
        return pltpu.VMEM((tiles, halves, high, SPAN, LANES), f32)

    return pl.pallas_call(
        functools.partial(kernel, nd, ns, tiles),
        out_shape=jax.ShapeDtypeStruct(initial_warmth.shape, f32),
        in_specs=[pl.BlockSpec(memory_space=pltpu.HBM)] * 5,
        out_specs=pl.BlockSpec(memory_space=pl.ANY),
        scratch_shapes=[
            pltpu.VMEM(labels.shape, labels.dtype),
            pltpu.SMEM(neighbour_kernel.shape, f32),
            pltpu.VMEM(arriving_heat_rate.shape, f32),
            pltpu.VMEM((layers, layers), f32),
            pltpu.VMEM((rows, layers_here, width), f32),
            pltpu.VMEM((tiles, rows, layers, LANES), f32),
            pltpu.VMEM((tiles, 2, rows, layers, LANES), f32),
            pltpu.VMEM((nd, layers_here, LANES), f32),
            pltpu.VMEM((layers, LANES), f32),
            pltpu.VMEM((halves, LANES, LANES), f32),
            pltpu.VMEM((2, halves, LANES, LANES), f32),
            pltpu.VMEM((2, rows, width), f32),
            state(rows + 8), state(rows + 4), state(rows + 4),
            pltpu.VMEM((rows + 4, (tiles + 2) * LANES, LANES), f32),
            pltpu.VMEM((rows + 4, WIDE, 2 * layers), jnp.bfloat16),
            pltpu.VMEM((tiles, rows, layers, LANES), f32),
            pltpu.VMEM((halves, 25, 8, LANES), f32),
            pltpu.VMEM((layers, 3 * layers), jnp.bfloat16),
            pltpu.VMEM((3 * layers, layers), jnp.bfloat16),
            dma((4,)), dma((rows,)),
            dma((nd, tiles + 1)), dma((nd, tiles + 1)), dma((tiles + 1,)),
            dma((2, nd, tiles)), dma((2, nd, tiles)), dma((2,)), dma((2,)), dma((2,)), dma((2,)),
            dma((tiles, 2, halves)), dma((tiles, 2, halves)),
            dma((nd, tiles, rows)), dma((nd, tiles, rows)), dma((tiles, rows)),
        ],
        compiler_params=pltpu.CompilerParams(
            collective_id=0, has_side_effects=True, vmem_limit_bytes=60 * 1024 * 1024
        ),
    )(initial_warmth, labels, neighbour_kernel, arriving_heat_rate, implicit_inverse_operator)


def solution(mesh):
    return jax.shard_map(
        functools.partial(shards, mesh.shape["depth"], mesh.shape["surf"]),
        mesh=mesh,
        in_specs=(P("depth", "surf", None), P(), P(), P("surf", None), P()),
        out_specs=P("depth", "surf", None),
        check_vma=False,
    )
```

```python
import functools

import jax
import jax.numpy as jnp
from jax import lax
from jax.experimental import pallas as pl
from jax.experimental.pallas import tpu as pltpu
from jax.sharding import PartitionSpec as P

LANES = 128
STRIP = 6
PAD = 16
SPAN = LANES + 2 * PAD
WIDE = LANES + 16
ROUND = 5
MESH = pl.DeviceIdType.MESH
NT = (((1,), (1,)), ((), ()))


def spread_rows(x):
    x0, x1, x2, x3, x4, x5, x6, x7 = x
    mid = 2.5 * x3
    e1, o1 = x2 + x6 - 4.25 * x4, x1 + x5 - 4.25 * x3
    e2, o2 = 0.25 * x2 - 1.25 * x4 + x6, 0.5 * x1 - mid + 2.0 * x5
    e3, o3 = 4.0 * x2 - 5.0 * x4 + x6, 2.0 * x1 - mid + 0.5 * x5
    return [
        x0 - x6 + 5.25 * (x4 - x2), e1 + o1, e1 - o1, e2 + o2, e2 - o2, e3 + o3, e3 - o3,
        x7 - x1 + 5.25 * (x3 - x5),
    ]


def spread_taps(c):
    c0, c1, c2, c3, c4 = c
    f1, f2, f3 = -2.0 / 9.0, 1.0 / 90.0, 32.0 / 45.0
    e1, o1 = c0 + c2 + c4, c1 + c3
    e2, o2 = c0 + 4.0 * c2 + 16.0 * c4, 2.0 * c1 + 8.0 * c3
    e3, o3 = c0 + 0.25 * c2 + 0.0625 * c4, 0.5 * c1 + 0.125 * c3
    return [
        c0, f1 * (e1 + o1), f1 * (e1 - o1), f2 * (e2 + o2), f2 * (e2 - o2),
        f3 * (e3 + o3), f3 * (e3 - o3), c4,
    ]


def gather_rows(m):
    s1, d1 = m[1] + m[2], m[1] - m[2]
    s2, d2 = m[3] + m[4], m[3] - m[4]
    s3, d3 = m[5] + m[6], m[5] - m[6]
    return [
        m[0] + s1 + s2 + s3, d1 + 2.0 * d2 + 0.5 * d3, s1 + 4.0 * s2 + 0.25 * s3,
        d1 + 8.0 * d2 + 0.125 * d3 + m[7],
    ]


def flipped(rank, mask, count):
    out, bit = 0, 1
    while bit < count:
        mine = (rank // bit) % 2
        out = out + bit * ((1 - mine) if (mask // bit) % 2 else mine)
        bit *= 2
    return out


def kernel(
    nd, ns, tiles,
    x_ref, lab_hbm, nk_hbm, heat_hbm, op_hbm, out_ref,
    lab_ref, nk_ref, heat_ref, op_ref,
    xr, raw, side_raw, eb, eraw, et, side_et, hb, s0, s1, s2, hot, wide, ex, ob, coef, op3, opt,
    i_sem, l_sem, a_send, a_recv, a_loc, f_send, f_recv, e_send, e_recv, h_send, h_recv,
    z_send, z_recv, o_send, o_recv, o_loc,
):
    d = lax.axis_index("depth")
    s = lax.axis_index("surf")
    layers_here, rows, width = x_ref.shape
    layers = op_ref.shape[0]
    halves = layers // LANES
    cols = tiles * LANES
    peers = [j for j in range(nd - 1, 0, -1)]
    has = (s > 0, s < ns - 1)
    near = (s - 1, s + 1)
    mine = pl.ds(pl.multiple_of(d * layers_here, 8), layers_here)

    def block_cols(b, t):
        return pl.ds(pl.multiple_of(b * cols + t * LANES, LANES), LANES)

    def fetch(k):
        src = (lab_hbm, nk_hbm, heat_hbm, op_hbm)[k]
        return pltpu.make_async_copy(src, (lab_ref, nk_ref, heat_ref, op_ref)[k], i_sem.at[k])

    def load(r):
        return pltpu.make_async_copy(x_ref.at[:, r, :], xr.at[r], l_sem.at[r])

    def spread(j, t):
        p = flipped(d, j, nd)
        if t == tiles:
            src, dst = eb.at[p], eraw.at[mine]
        else:
            src, dst = xr.at[:, :, block_cols(p, t)], raw.at[t, :, mine]
        return pltpu.make_async_remote_copy(
            src, dst, a_send.at[j, t], a_recv.at[j, t],
            device_id={"depth": p}, device_id_type=MESH,
        )

    def keep(t):
        if t == tiles:
            src, dst = eb.at[d], eraw.at[mine]
        else:
            src, dst = xr.at[:, :, block_cols(d, t)], raw.at[t, :, mine]
        return pltpu.make_async_copy(src, dst, a_loc.at[t])

    def forward(side, j, t):
        p = flipped(d, j, nd)
        part = pl.ds(pl.multiple_of(p * layers_here, 8), layers_here)
        src = raw.at[t, :, part] if j else xr.at[:, :, block_cols(d, t)]
        return pltpu.make_async_remote_copy(
            src, side_raw.at[t, 1 - side, :, part], f_send.at[side, j, t], f_recv.at[side, j, t],
            device_id={"surf": near[side]}, device_id_type=MESH,
        )

    def forward_strips(side):
        return pltpu.make_async_remote_copy(
            et, side_et.at[1 - side], e_send.at[side], e_recv.at[side],
            device_id={"surf": near[side]}, device_id_type=MESH,
        )

    def heat_out(side):
        return pltpu.make_async_remote_copy(
            heat_hbm, hb.at[1 - side], h_send.at[side], h_recv.at[side],
            device_id={"surf": near[side]}, device_id_type=MESH,
        )

    def trade(t, side, h):
        part = pl.ds(PAD - 2, LANES + 4)
        return pltpu.make_async_remote_copy(
            s2.at[t, h, pl.ds(2 + 2 * side, 2), part],
            s2.at[t, h, pl.ds(6 - 6 * side, 2), part],
            z_send.at[t, side, h], z_recv.at[t, side, h],
            device_id={"surf": near[side]}, device_id_type=MESH,
        )

    def at_sides(action):
        for side in range(2):
            @pl.when(has[side])
            def _():
                action(side)

    def give_back(j, t, r):
        p = flipped(d, j, nd)
        theirs = pl.ds(pl.multiple_of(p * layers_here, 8), layers_here)
        return pltpu.make_async_remote_copy(
            ob.at[t, r, theirs], out_ref.at[:, r, block_cols(d, t)],
            o_send.at[j, t, r], o_recv.at[j, t, r],
            device_id={"depth": p}, device_id_type=MESH,
        )

    def put_home(t, r):
        return pltpu.make_async_copy(
            ob.at[t, r, mine], out_ref.at[:, r, block_cols(d, t)], o_loc.at[t, r]
        )

    barrier = pltpu.get_barrier_semaphore()
    for j in peers:
        pl.semaphore_signal(
            barrier, inc=1, device_id={"depth": flipped(d, j, nd)}, device_id_type=MESH
        )
    for side in range(2):
        @pl.when(has[side])
        def _():
            pl.semaphore_signal(
                barrier, inc=1, device_id={"surf": near[side]}, device_id_type=MESH
            )
    at_end = jnp.where(s > 0, 0, 1) + jnp.where(s < ns - 1, 0, 1)
    for r in range(rows):
        load(r).start()
    for k in range(4):
        fetch(k).start()
    for r in range(rows):
        load(r).wait()
    pl.semaphore_wait(barrier, nd + 1 - at_end)

    own = 2
    spread(peers[0], 0).start()
    def first_sends(side):
        forward(side, 0, 0).start()
        heat_out(side).start()
        for t in range(1, min(own, tiles)):
            forward(side, 0, t).start()

    at_sides(first_sends)

    lane8 = lax.broadcasted_iota(jnp.int32, (8, LANES), 1)
    group = LANES // rows
    for b in range(nd):
        @pl.loop(0, layers_here // 8)
        def _(g):
            part = pl.ds(pl.multiple_of(g * 8, 8), 8)
            packed = jnp.zeros((8, LANES), jnp.float32)
            for r in range(rows):
                edge = jnp.zeros((8, LANES), jnp.float32)
                for i in range(tiles):
                    at = b * cols + (i + 1) * LANES
                    if at < width:
                        v = xr[r, part, at:at + LANES]
                        v = jnp.where(lane8 < STRIP, v, 0.0)
                        shift = STRIP * i + group * r
                        edge = edge + (pltpu.roll(v, shift, 1) if shift else v)
                if b > 0:
                    v = xr[r, part, b * cols - LANES:b * cols]
                    v = jnp.where(lane8 >= LANES - STRIP, v, 0.0)
                    shift = (group * (r + 1)) % LANES
                    edge = edge + (pltpu.roll(v, shift, 1) if shift else v)
                packed = packed + edge
            eb[b, part, :] = packed
    for j in peers:
        spread(j, tiles).start()
    for j in peers[1:]:
        spread(j, 0).start()
    for t in range(1, tiles):
        for j in peers:
            spread(j, t).start()
    for t in range(tiles + 1):
        keep(t).start()

    for k in range(4):
        fetch(k).wait()
    for h in range(halves):
        kind = jnp.broadcast_to(lab_ref[:, h * LANES:(h + 1) * LANES], (8, LANES))
        total = jnp.zeros((8, LANES), jnp.float32)
        taps = []
        for k in range(24):
            c = jnp.where(
                kind == 0, nk_ref[0, k],
                jnp.where(kind == 1, nk_ref[1, k], jnp.where(kind == 2, nk_ref[2, k], nk_ref[3, k])),
            )
            taps.append(c)
            total = total + c
        taps.insert(12, 1.0 - total)
        for q in range(5):
            for i, c in enumerate(spread_taps(taps[q::5])):
                coef[h, i * 5 + q] = c

    high = op_ref[...].astype(jnp.bfloat16)
    low = (op_ref[...] - high.astype(jnp.float32)).astype(jnp.bfloat16)
    op3[:, 0:layers] = high
    op3[:, layers:2 * layers] = high
    op3[:, 2 * layers:] = low
    turned = jnp.transpose(op_ref[...])
    high = turned.astype(jnp.bfloat16)
    low = (turned - high.astype(jnp.float32)).astype(jnp.bfloat16)
    opt[0:layers, :] = high
    opt[layers:2 * layers, :] = high
    opt[2 * layers:, :] = low

    top = lax.broadcasted_iota(jnp.int32, (LANES, LANES), 0) == 0

    def heat_row(src, row, to):
        for t in range(-1, tiles + 1):
            b = d if 0 <= t < tiles else (lax.rem(d + nd - 1, nd) if t < 0 else lax.rem(d + 1, nd))
            line = src[row:row + 1, block_cols(b, t % tiles)]
            tall = jnp.transpose(jnp.where(top, jnp.broadcast_to(line, (LANES, LANES)), 0.0))
            hot[to, (t + 1) * LANES:(t + 2) * LANES, :] = tall

    for r in range(rows):
        heat_row(heat_ref, r, 2 + r)

    for side in range(2):
        @pl.when(jnp.logical_not(has[side]))
        def _():
            @pl.loop(0, tiles)
            def _(t):
                for h in range(halves):
                    for r in range(rows):
                        s0[t, h, 8 * side + r] = jnp.zeros((SPAN, LANES), jnp.float32)
                    for r in range(2):
                        s2[t, h, 6 * side + r] = jnp.zeros((SPAN, LANES), jnp.float32)

    def side_heat(side):
        heat_out(1 - side).wait_recv()
        for r in range(2):
            heat_row(hb.at[side], r + 2 - 2 * side, r + 6 * side)

    at_sides(side_heat)

    def lateral(src, t, first, groups, made, warm, ready=None):
        sets = made // 4
        for h in range(halves):
            if ready is not None:
                ready(h)

            turns = (groups + 2) // ROUND

            @pl.loop(0, turns)
            def _(g):
                for u in range(ROUND):
                    here = pl.ds(pl.multiple_of(first - 8 + (g * ROUND + u) * 8, 8), 8)
                    for k in range(sets):
                        v = spread_rows([src[t, h, 4 * k + i, here, :] for i in range(8)])
                        for i in range(8):
                            wide[k, i, here, :] = v[i]

            for u in range(turns * ROUND, groups + 2):
                here = pl.ds(first - 8 + u * 8, 8)
                for k in range(sets):
                    v = spread_rows([src[t, h, 4 * k + i, here, :] for i in range(8)])
                    for i in range(8):
                        wide[k, i, here, :] = v[i]

            per = 3 if groups % 6 == 0 else 4

            @pl.loop(0, groups // (2 * per))
            def _(g):
                for w in range(per):
                    at = pl.multiple_of(first + (g * per + w) * 16, 8)
                    parts = [[[] for _ in range(sets)] for _ in range(2)]
                    for i in range(8):
                        cs = [coef[h, i * 5 + q] for q in range(5)]
                        for u in range(2):
                            for k in range(sets):
                                m = None
                                for q in range(5):
                                    term = cs[q] * wide[k, i, pl.ds(at + 8 * u + q - 2, 8), :]
                                    m = term if m is None else m + term
                                parts[u][k].append(m)
                    here = pl.ds(pl.multiple_of((g * per + w) * 16, 16), 16)
                    for k in range(sets):
                        both = [gather_rows(parts[u][k]) for u in range(2)]
                        for r in range(4 * k, 4 * k + 4):
                            v = jnp.concatenate([both[0][r - 4 * k], both[1][r - 4 * k]], axis=0)
                            if h == 0:
                                v = v + hot[warm + r, pl.ds(at + (t + 1) * LANES - PAD, 16), :]
                            eh = v.astype(jnp.bfloat16)
                            el = (v - eh.astype(jnp.float32)).astype(jnp.bfloat16)
                            ex[r, here, h * LANES:(h + 1) * LANES] = eh
                            ex[r, here, layers + h * LANES:layers + (h + 1) * LANES] = el

    def implicit(t, dst, made, to):
        for r in range(made):
            e = ex[r]
            y = jnp.dot(
                jnp.concatenate([e, e[:, :layers]], axis=1), opt[...],
                preferred_element_type=jnp.float32,
            )
            for h in range(halves):
                dst[t, h, to + r, PAD - 8:PAD - 8 + WIDE, :] = y[:, h * LANES:(h + 1) * LANES]
        for at, edge in ((PAD - 8, jnp.logical_and(t == 0, d == 0)),
                         (PAD + LANES, jnp.logical_and(t == tiles - 1, d == nd - 1))):
            if t not in (0, tiles - 1):
                continue

            @pl.when(edge)
            def _():
                for h in range(halves):
                    for r in range(made):
                        dst[t, h, to + r, at:at + 8, :] = jnp.zeros((8, LANES), jnp.float32)

    def receive(t, k):
        for j in (peers[k:k + 1] if k < 2 else peers[2:]):
            spread(j, t).wait_recv()
            at_sides(lambda side: forward(side, j, t).start())
        if t == 0 and k == 0:
            for j in peers:
                spread(j, tiles).wait_recv()
            keep(tiles).wait()
            for h in range(halves):
                et[h] = jnp.transpose(eraw[h * LANES:(h + 1) * LANES, :])
            at_sides(lambda side: forward_strips(side).start())
        if k == 2 and t + own < tiles:
            at_sides(lambda side: forward(side, 0, t + own).start())

    def unpack(t, src, strips, row, to):
        for h in range(halves):
            s0[t, h, to, PAD:PAD + LANES, :] = jnp.transpose(
                src[row, h * LANES:(h + 1) * LANES, :]
            )
            if t == 0:
                left = strips[h, group * (row + 1) - 8:group * (row + 1), :]
            else:
                left = s0[t - 1, h, to, PAD + LANES - 8:PAD + LANES, :]
            s0[t, h, to, PAD - 8:PAD, :] = left
            at = group * row + STRIP * t
            s0[t, h, to, PAD + LANES:PAD + LANES + 8, :] = strips[h, at:at + 8, :]

    def arrange(t):
        keep(t).wait()
        for r in range(rows):
            unpack(t, raw.at[t], et, r, rows + r)

    def arrange_side(t):
        def one(side):
            if t == 0:
                forward_strips(1 - side).wait_recv()
            for j in range(nd):
                forward(1 - side, j, t).wait_recv()
            for r in range(rows):
                unpack(t, side_raw.at[t, side], side_et.at[side], r, 2 * rows * side + r)

        at_sides(one)

    def step1(t):
        lateral(s0, t, PAD - 8, WIDE // 8, rows + 4, 0)
        implicit(t, s1, rows + 4, 0)
        for side in range(2):
            @pl.when(jnp.logical_not(has[side]))
            def _():
                for h in range(halves):
                    for r in range(2):
                        s1[t, h, 6 * side + r] = jnp.zeros((SPAN, LANES), jnp.float32)

    def step2(t):
        lateral(s1, t, PAD - 8, WIDE // 8, rows, 2)
        implicit(t, s2, rows, 2)
        for h in range(halves):
            at_sides(lambda side: trade(t, side, h).start())

    def last(t):
        def ready(h):
            at_sides(lambda side: trade(t, 1 - side, h).wait_recv())

        lateral(s2, t, PAD, LANES // 8, rows, 2, ready)
        for pair in range(rows // 2):
            e = jnp.concatenate([ex[2 * pair, 0:LANES], ex[2 * pair + 1, 0:LANES]], axis=0)
            y = lax.dot_general(
                op3[...], jnp.concatenate([e, e[:, :layers]], axis=1), NT,
                preferred_element_type=jnp.float32,
            )
            for r in range(2 * pair, 2 * pair + 2):
                ob[t, r] = y[:, (r % 2) * LANES:(r % 2 + 1) * LANES]
                for j in peers:
                    give_back(j, t, r).start()
                put_home(t, r).start()

    plan = (
        "P0", "Q0", "R0", "P1", "Q1", "a0", "h0", "R1", "10", "a1", "P2",
        "20", "h1", "11", "Q2", "R2", "21", "P3", "Q3", "30", "a2", "h2",
        "R3", "12", "31", "a3", "22", "h3", "13", "23", "32", "33",
    )
    for item in plan:
        t = int(item[1])
        if t < tiles:
            {
                "P": lambda: receive(t, 0), "Q": lambda: receive(t, 1), "R": lambda: receive(t, 2),
                "a": lambda: arrange(t), "h": lambda: arrange_side(t),
                "1": lambda: step1(t), "2": lambda: step2(t), "3": lambda: last(t),
            }[item[0]]()

    for t in range(tiles):
        for r in range(rows):
            for j in peers:
                give_back(j, t, r).wait()
            put_home(t, r).wait()
    for t in range(tiles + 1):
        for j in peers:
            spread(j, t).wait_send()
    def sent(side):
        forward_strips(side).wait_send()
        heat_out(side).wait_send()
        for t in range(tiles):
            for j in range(nd):
                forward(side, j, t).wait_send()
            for h in range(halves):
                trade(t, side, h).wait_send()

    at_sides(sent)


def shards(
    nd, ns,
    initial_warmth, substance_label, neighbour_kernel, arriving_heat_rate, implicit_inverse_operator,
):
    layers_here, rows, width = initial_warmth.shape
    layers = implicit_inverse_operator.shape[0]
    tiles = width // nd // LANES
    halves = layers // LANES
    labels = substance_label[None, :]
    f32, dma = jnp.float32, pltpu.SemaphoreType.DMA

    def state(high):
        return pltpu.VMEM((tiles, halves, high, SPAN, LANES), f32)

    return settled(pl.pallas_call(
        functools.partial(kernel, nd, ns, tiles),
        out_shape=jax.ShapeDtypeStruct(initial_warmth.shape, f32),
        in_specs=[pl.BlockSpec(memory_space=pltpu.HBM)] * 5,
        out_specs=pl.BlockSpec(memory_space=pl.ANY),
        scratch_shapes=[
            pltpu.VMEM(labels.shape, labels.dtype),
            pltpu.SMEM(neighbour_kernel.shape, f32),
            pltpu.VMEM(arriving_heat_rate.shape, f32),
            pltpu.VMEM((layers, layers), f32),
            pltpu.VMEM((rows, layers_here, width), f32),
            pltpu.VMEM((tiles, rows, layers, LANES), f32),
            pltpu.VMEM((tiles, 2, rows, layers, LANES), f32),
            pltpu.VMEM((nd, layers_here, LANES), f32),
            pltpu.VMEM((layers, LANES), f32),
            pltpu.VMEM((halves, LANES, LANES), f32),
            pltpu.VMEM((2, halves, LANES, LANES), f32),
            pltpu.VMEM((2, rows, width), f32),
            state(rows + 8), state(rows + 4), state(rows + 4),
            pltpu.VMEM((rows + 4, (tiles + 2) * LANES, LANES), f32),
            pltpu.VMEM(((rows + 4) // 4, 8, SPAN, LANES), f32),
            pltpu.VMEM((rows + 4, WIDE, 2 * layers), jnp.bfloat16),
            pltpu.VMEM((tiles, rows, layers, LANES), f32),
            pltpu.VMEM((halves, 40, 8, LANES), f32),
            pltpu.VMEM((layers, 3 * layers), jnp.bfloat16),
            pltpu.VMEM((3 * layers, layers), jnp.bfloat16),
            dma((4,)), dma((rows,)),
            dma((nd, tiles + 1)), dma((nd, tiles + 1)), dma((tiles + 1,)),
            dma((2, nd, tiles)), dma((2, nd, tiles)), dma((2,)), dma((2,)), dma((2,)), dma((2,)),
            dma((tiles, 2, halves)), dma((tiles, 2, halves)),
            dma((nd, tiles, rows)), dma((nd, tiles, rows)), dma((tiles, rows)),
        ],
        compiler_params=pltpu.CompilerParams(
            collective_id=0, has_side_effects=True, vmem_limit_bytes=60 * 1024 * 1024
        ),
    )(initial_warmth, labels, neighbour_kernel, arriving_heat_rate, implicit_inverse_operator))


def settle(src_ref, out_ref, buf, i_sem, o_sem):
    pieces = i_sem.shape[0]
    each = src_ref.shape[0] // pieces

    def copy(k, out):
        part = pl.ds(k * each, each)
        if out:
            return pltpu.make_async_copy(buf.at[part], out_ref.at[part], o_sem.at[k])
        return pltpu.make_async_copy(src_ref.at[part], buf.at[part], i_sem.at[k])

    for k in range(pieces):
        copy(k, False).start()
    for k in range(pieces):
        copy(k, False).wait()
        copy(k, True).start()
    for k in range(pieces):
        copy(k, True).wait()


def settled(x):
    pieces = 8
    hbm = pl.BlockSpec(memory_space=pltpu.HBM)
    return pl.pallas_call(
        settle,
        out_shape=jax.ShapeDtypeStruct(x.shape, x.dtype),
        in_specs=[hbm],
        out_specs=hbm,
        scratch_shapes=[
            pltpu.VMEM(x.shape, x.dtype),
            pltpu.SemaphoreType.DMA((pieces,)), pltpu.SemaphoreType.DMA((pieces,)),
        ],
        compiler_params=pltpu.CompilerParams(vmem_limit_bytes=60 * 1024 * 1024),
    )(x)


def solution(mesh):
    return jax.shard_map(
        functools.partial(shards, mesh.shape["depth"], mesh.shape["surf"]),
        mesh=mesh,
        in_specs=(P("depth", "surf", None), P(), P(), P("surf", None), P()),
        out_specs=P("depth", "surf", None),
        check_vma=False,
    )
```

```python
import functools

import jax
import jax.numpy as jnp
from jax import lax
from jax.experimental import pallas as pl
from jax.experimental.pallas import tpu as pltpu
from jax.sharding import PartitionSpec as P

LANES = 128
STRIP = 6
PAD = 16
SPAN = LANES + 2 * PAD
WIDE = LANES + 16
ROUND = 5
MESH = pl.DeviceIdType.MESH
NT = (((1,), (1,)), ((), ()))


def spread_rows(x):
    x0, x1, x2, x3, x4, x5, x6, x7 = x
    mid = 2.5 * x3
    e1, o1 = x2 + x6 - 4.25 * x4, x1 + x5 - 4.25 * x3
    e2, o2 = 0.25 * x2 - 1.25 * x4 + x6, 0.5 * x1 - mid + 2.0 * x5
    e3, o3 = 4.0 * x2 - 5.0 * x4 + x6, 2.0 * x1 - mid + 0.5 * x5
    return [
        x0 - x6 + 5.25 * (x4 - x2), e1 + o1, e1 - o1, e2 + o2, e2 - o2, e3 + o3, e3 - o3,
        x7 - x1 + 5.25 * (x3 - x5),
    ]


def spread_taps(c):
    c0, c1, c2, c3, c4 = c
    f1, f2, f3 = -2.0 / 9.0, 1.0 / 90.0, 32.0 / 45.0
    e1, o1 = c0 + c2 + c4, c1 + c3
    e2, o2 = c0 + 4.0 * c2 + 16.0 * c4, 2.0 * c1 + 8.0 * c3
    e3, o3 = c0 + 0.25 * c2 + 0.0625 * c4, 0.5 * c1 + 0.125 * c3
    return [
        c0, f1 * (e1 + o1), f1 * (e1 - o1), f2 * (e2 + o2), f2 * (e2 - o2),
        f3 * (e3 + o3), f3 * (e3 - o3), c4,
    ]


def gather_rows(m):
    s1, d1 = m[1] + m[2], m[1] - m[2]
    s2, d2 = m[3] + m[4], m[3] - m[4]
    s3, d3 = m[5] + m[6], m[5] - m[6]
    return [
        m[0] + s1 + s2 + s3, d1 + 2.0 * d2 + 0.5 * d3, s1 + 4.0 * s2 + 0.25 * s3,
        d1 + 8.0 * d2 + 0.125 * d3 + m[7],
    ]


def flipped(rank, mask, count):
    out, bit = 0, 1
    while bit < count:
        mine = (rank // bit) % 2
        out = out + bit * ((1 - mine) if (mask // bit) % 2 else mine)
        bit *= 2
    return out


def kernel(
    nd, ns, tiles,
    x_ref, lab_hbm, nk_hbm, heat_hbm, op_hbm, out_ref,
    lab_ref, nk_ref, heat_ref, op_ref,
    xr, raw, side_raw, eb, eraw, et, side_et, hb, s0, s1, s2, hot, wide, ex, ob, coef, op3, opt,
    i_sem, l_sem, a_send, a_recv, a_loc, f_send, f_recv, e_send, e_recv, h_send, h_recv,
    z_send, z_recv, o_send, o_recv, o_loc,
):
    d = lax.axis_index("depth")
    s = lax.axis_index("surf")
    layers_here, rows, width = x_ref.shape
    layers = op_ref.shape[0]
    halves = layers // LANES
    cols = tiles * LANES
    peers = [j for j in range(nd - 1, 0, -1)]
    has = (s > 0, s < ns - 1)
    near = (s - 1, s + 1)
    mine = pl.ds(pl.multiple_of(d * layers_here, 8), layers_here)

    def block_cols(b, t):
        return pl.ds(pl.multiple_of(b * cols + t * LANES, LANES), LANES)

    def fetch(k):
        src = (lab_hbm, nk_hbm, heat_hbm, op_hbm)[k]
        return pltpu.make_async_copy(src, (lab_ref, nk_ref, heat_ref, op_ref)[k], i_sem.at[k])

    def load(r):
        return pltpu.make_async_copy(x_ref.at[:, r, :], xr.at[r], l_sem.at[r])

    def spread(j, t):
        p = flipped(d, j, nd)
        if t == tiles:
            src, dst = eb.at[p], eraw.at[mine]
        else:
            src, dst = xr.at[:, :, block_cols(p, t)], raw.at[t, :, mine]
        return pltpu.make_async_remote_copy(
            src, dst, a_send.at[j, t], a_recv.at[j, t],
            device_id={"depth": p}, device_id_type=MESH,
        )

    def keep(t):
        if t == tiles:
            src, dst = eb.at[d], eraw.at[mine]
        else:
            src, dst = xr.at[:, :, block_cols(d, t)], raw.at[t, :, mine]
        return pltpu.make_async_copy(src, dst, a_loc.at[t])

    def forward(side, j, t):
        p = flipped(d, j, nd)
        part = pl.ds(pl.multiple_of(p * layers_here, 8), layers_here)
        src = raw.at[t, :, part] if j else xr.at[:, :, block_cols(d, t)]
        return pltpu.make_async_remote_copy(
            src, side_raw.at[t, 1 - side, :, part], f_send.at[side, j, t], f_recv.at[side, j, t],
            device_id={"surf": near[side]}, device_id_type=MESH,
        )

    def forward_strips(side):
        return pltpu.make_async_remote_copy(
            et, side_et.at[1 - side], e_send.at[side], e_recv.at[side],
            device_id={"surf": near[side]}, device_id_type=MESH,
        )

    def heat_out(side):
        return pltpu.make_async_remote_copy(
            heat_hbm, hb.at[1 - side], h_send.at[side], h_recv.at[side],
            device_id={"surf": near[side]}, device_id_type=MESH,
        )

    def trade(t, side, h):
        part = pl.ds(PAD - 2, LANES + 4)
        return pltpu.make_async_remote_copy(
            s2.at[t, h, pl.ds(2 + 2 * side, 2), part],
            s2.at[t, h, pl.ds(6 - 6 * side, 2), part],
            z_send.at[t, side, h], z_recv.at[t, side, h],
            device_id={"surf": near[side]}, device_id_type=MESH,
        )

    def at_sides(action):
        for side in range(2):
            @pl.when(has[side])
            def _():
                action(side)

    def give_back(j, t, r):
        p = flipped(d, j, nd)
        theirs = pl.ds(pl.multiple_of(p * layers_here, 8), layers_here)
        return pltpu.make_async_remote_copy(
            ob.at[t, r, theirs], out_ref.at[:, r, block_cols(d, t)],
            o_send.at[j, t, r], o_recv.at[j, t, r],
            device_id={"depth": p}, device_id_type=MESH,
        )

    def put_home(t, r):
        return pltpu.make_async_copy(
            ob.at[t, r, mine], out_ref.at[:, r, block_cols(d, t)], o_loc.at[t, r]
        )

    barrier = pltpu.get_barrier_semaphore()
    for j in peers:
        pl.semaphore_signal(
            barrier, inc=1, device_id={"depth": flipped(d, j, nd)}, device_id_type=MESH
        )
    for side in range(2):
        @pl.when(has[side])
        def _():
            pl.semaphore_signal(
                barrier, inc=1, device_id={"surf": near[side]}, device_id_type=MESH
            )
    at_end = jnp.where(s > 0, 0, 1) + jnp.where(s < ns - 1, 0, 1)
    for r in range(rows):
        load(r).start()
    for k in range(4):
        fetch(k).start()
    for r in range(rows):
        load(r).wait()
    pl.semaphore_wait(barrier, nd + 1 - at_end)

    own = 2
    spread(peers[0], 0).start()
    def first_sends(side):
        forward(side, 0, 0).start()
        heat_out(side).start()
        for t in range(1, min(own, tiles)):
            forward(side, 0, t).start()

    at_sides(first_sends)

    lane8 = lax.broadcasted_iota(jnp.int32, (8, LANES), 1)
    group = LANES // rows
    for b in range(nd):
        @pl.loop(0, layers_here // 8)
        def _(g):
            part = pl.ds(pl.multiple_of(g * 8, 8), 8)
            packed = jnp.zeros((8, LANES), jnp.float32)
            for r in range(rows):
                edge = jnp.zeros((8, LANES), jnp.float32)
                for i in range(tiles):
                    at = b * cols + (i + 1) * LANES
                    if at < width:
                        v = xr[r, part, at:at + LANES]
                        v = jnp.where(lane8 < STRIP, v, 0.0)
                        shift = STRIP * i + group * r
                        edge = edge + (pltpu.roll(v, shift, 1) if shift else v)
                if b > 0:
                    v = xr[r, part, b * cols - LANES:b * cols]
                    v = jnp.where(lane8 >= LANES - STRIP, v, 0.0)
                    shift = (group * (r + 1)) % LANES
                    edge = edge + (pltpu.roll(v, shift, 1) if shift else v)
                packed = packed + edge
            eb[b, part, :] = packed
    for j in peers:
        spread(j, tiles).start()
    for j in peers[1:]:
        spread(j, 0).start()
    for t in range(1, tiles):
        for j in peers:
            spread(j, t).start()
    for t in range(tiles + 1):
        keep(t).start()

    for k in range(4):
        fetch(k).wait()
    for h in range(halves):
        kind = jnp.broadcast_to(lab_ref[:, h * LANES:(h + 1) * LANES], (8, LANES))
        total = jnp.zeros((8, LANES), jnp.float32)
        taps = []
        for k in range(24):
            c = jnp.where(
                kind == 0, nk_ref[0, k],
                jnp.where(kind == 1, nk_ref[1, k], jnp.where(kind == 2, nk_ref[2, k], nk_ref[3, k])),
            )
            taps.append(c)
            total = total + c
        taps.insert(12, 1.0 - total)
        for q in range(5):
            for i, c in enumerate(spread_taps(taps[q::5])):
                coef[h, i * 5 + q] = c

    high = op_ref[...].astype(jnp.bfloat16)
    low = (op_ref[...] - high.astype(jnp.float32)).astype(jnp.bfloat16)
    op3[:, 0:layers] = high
    op3[:, layers:2 * layers] = high
    op3[:, 2 * layers:] = low
    turned = jnp.transpose(op_ref[...])
    high = turned.astype(jnp.bfloat16)
    low = (turned - high.astype(jnp.float32)).astype(jnp.bfloat16)
    opt[0:layers, :] = high
    opt[layers:2 * layers, :] = high
    opt[2 * layers:, :] = low

    top = lax.broadcasted_iota(jnp.int32, (LANES, LANES), 0) == 0

    def heat_row(src, row, to):
        for t in range(-1, tiles + 1):
            b = d if 0 <= t < tiles else (lax.rem(d + nd - 1, nd) if t < 0 else lax.rem(d + 1, nd))
            line = src[row:row + 1, block_cols(b, t % tiles)]
            tall = jnp.transpose(jnp.where(top, jnp.broadcast_to(line, (LANES, LANES)), 0.0))
            hot[to, (t + 1) * LANES:(t + 2) * LANES, :] = tall

    for r in range(rows):
        heat_row(heat_ref, r, 2 + r)

    for side in range(2):
        @pl.when(jnp.logical_not(has[side]))
        def _():
            @pl.loop(0, tiles)
            def _(t):
                for h in range(halves):
                    for r in range(rows):
                        s0[t, h, 8 * side + r] = jnp.zeros((SPAN, LANES), jnp.float32)
                    for r in range(2):
                        s2[t, h, 6 * side + r] = jnp.zeros((SPAN, LANES), jnp.float32)

    def side_heat(side):
        heat_out(1 - side).wait_recv()
        for r in range(2):
            heat_row(hb.at[side], r + 2 - 2 * side, r + 6 * side)

    at_sides(side_heat)

    def lateral(src, t, first, groups, made, warm, ready=None):
        sets = made // 4
        for h in range(halves):
            if ready is not None:
                ready(h)

            def widen(u):
                for k in range(sets):
                    there = pl.ds(first - 2 + u * 8, 8)
                    v = spread_rows([src[t, h, 4 * k + i, there, :] for i in range(8)])
                    for i in range(8):
                        wide[k, i, pl.ds(pl.multiple_of(u * 8, 8), 8), :] = v[i]

            turns = (groups + 1) // ROUND

            @pl.loop(0, turns)
            def _(g):
                for u in range(ROUND):
                    widen(g * ROUND + u)

            for u in range(turns * ROUND, groups + 1):
                widen(u)

            per = 3 if groups % 6 == 0 else 4

            @pl.loop(0, groups // (2 * per))
            def _(g):
                for w in range(per):
                    at = pl.multiple_of((g * per + w) * 16, 16)
                    parts = [[[] for _ in range(sets)] for _ in range(2)]
                    for i in range(8):
                        cs = [coef[h, i * 5 + q] for q in range(5)]
                        for u in range(2):
                            for k in range(sets):
                                m = None
                                for q in range(5):
                                    term = cs[q] * wide[k, i, pl.ds(at + 8 * u + q, 8), :]
                                    m = term if m is None else m + term
                                parts[u][k].append(m)
                    here = pl.ds(pl.multiple_of((g * per + w) * 16, 16), 16)
                    for k in range(sets):
                        both = [gather_rows(parts[u][k]) for u in range(2)]
                        for r in range(4 * k, 4 * k + 4):
                            v = jnp.concatenate([both[0][r - 4 * k], both[1][r - 4 * k]], axis=0)
                            if h == 0:
                                v = v + hot[warm + r, pl.ds(at + first + (t + 1) * LANES - PAD, 16), :]
                            eh = v.astype(jnp.bfloat16)
                            el = (v - eh.astype(jnp.float32)).astype(jnp.bfloat16)
                            ex[r, here, h * LANES:(h + 1) * LANES] = eh
                            ex[r, here, layers + h * LANES:layers + (h + 1) * LANES] = el

    def implicit(t, dst, made, to, first, count):
        for r in range(made):
            e = ex[r, 0:count]
            y = jnp.dot(
                jnp.concatenate([e, e[:, :layers]], axis=1), opt[...],
                preferred_element_type=jnp.float32,
            )
            for h in range(halves):
                dst[t, h, to + r, first:first + count, :] = y[:, h * LANES:(h + 1) * LANES]
                if t:
                    old = dst[t - 1, h, to + r, first + LANES - 8:first + LANES, :]
                    dst[t, h, to + r, first - 8:first, :] = old
        for at, edge in ((PAD - 8, jnp.logical_and(t == 0, d == 0)),
                         (PAD + LANES, jnp.logical_and(t == tiles - 1, d == nd - 1))):
            if t not in (0, tiles - 1):
                continue

            @pl.when(edge)
            def _():
                for h in range(halves):
                    for r in range(made):
                        dst[t, h, to + r, at:at + 8, :] = jnp.zeros((8, LANES), jnp.float32)

    def receive(t, k):
        for j in (peers[k:k + 1] if k < 2 else peers[2:]):
            spread(j, t).wait_recv()
            at_sides(lambda side: forward(side, j, t).start())
        if t == 0 and k == 0:
            for j in peers:
                spread(j, tiles).wait_recv()
            keep(tiles).wait()
            for h in range(halves):
                et[h] = jnp.transpose(eraw[h * LANES:(h + 1) * LANES, :])
            at_sides(lambda side: forward_strips(side).start())
        if k == 2 and t + own < tiles:
            at_sides(lambda side: forward(side, 0, t + own).start())

    def unpack(t, src, strips, row, to):
        for h in range(halves):
            s0[t, h, to, PAD:PAD + LANES, :] = jnp.transpose(
                src[row, h * LANES:(h + 1) * LANES, :]
            )
            if t == 0:
                left = strips[h, group * (row + 1) - 8:group * (row + 1), :]
            else:
                left = s0[t - 1, h, to, PAD + LANES - 8:PAD + LANES, :]
            s0[t, h, to, PAD - 8:PAD, :] = left
            at = group * row + STRIP * t
            s0[t, h, to, PAD + LANES:PAD + LANES + 8, :] = strips[h, at:at + 8, :]

    def arrange(t):
        keep(t).wait()
        for r in range(rows):
            unpack(t, raw.at[t], et, r, rows + r)

    def arrange_side(t):
        def one(side):
            if t == 0:
                forward_strips(1 - side).wait_recv()
            for j in range(nd):
                forward(1 - side, j, t).wait_recv()
            for r in range(rows):
                unpack(t, side_raw.at[t, side], side_et.at[side], r, 2 * rows * side + r)

        at_sides(one)

    def advance(src, t, made, warm, dst, to, reach):
        count = LANES if t else WIDE
        first = PAD + LANES + reach - count
        lateral(src, t, first, count // 8, made, warm)
        implicit(t, dst, made, to, first, count)

    def step1(t):
        advance(s0, t, rows + 4, 0, s1, 0, 4)
        for side in range(2):
            @pl.when(jnp.logical_not(has[side]))
            def _():
                for h in range(halves):
                    for r in range(2):
                        s1[t, h, 6 * side + r] = jnp.zeros((SPAN, LANES), jnp.float32)

    def step2(t):
        advance(s1, t, rows, 2, s2, 2, 2)
        for h in range(halves):
            at_sides(lambda side: trade(t, side, h).start())

    def last(t):
        def ready(h):
            at_sides(lambda side: trade(t, 1 - side, h).wait_recv())

        lateral(s2, t, PAD, LANES // 8, rows, 2, ready)
        for pair in range(rows // 2):
            e = jnp.concatenate([ex[2 * pair, 0:LANES], ex[2 * pair + 1, 0:LANES]], axis=0)
            y = lax.dot_general(
                op3[...], jnp.concatenate([e, e[:, :layers]], axis=1), NT,
                preferred_element_type=jnp.float32,
            )
            for r in range(2 * pair, 2 * pair + 2):
                ob[t, r] = y[:, (r % 2) * LANES:(r % 2 + 1) * LANES]
                for j in peers:
                    give_back(j, t, r).start()
                put_home(t, r).start()

    plan = (
        "P0", "Q0", "R0", "P1", "Q1", "a0", "h0", "R1", "10", "a1", "P2",
        "20", "h1", "11", "Q2", "R2", "21", "P3", "Q3", "30", "a2", "h2",
        "R3", "12", "31", "a3", "22", "h3", "13", "23", "32", "33",
    )
    for item in plan:
        t = int(item[1])
        if t < tiles:
            {
                "P": lambda: receive(t, 0), "Q": lambda: receive(t, 1), "R": lambda: receive(t, 2),
                "a": lambda: arrange(t), "h": lambda: arrange_side(t),
                "1": lambda: step1(t), "2": lambda: step2(t), "3": lambda: last(t),
            }[item[0]]()

    for t in range(tiles):
        for r in range(rows):
            for j in peers:
                give_back(j, t, r).wait()
            put_home(t, r).wait()
    for t in range(tiles + 1):
        for j in peers:
            spread(j, t).wait_send()
    def sent(side):
        forward_strips(side).wait_send()
        heat_out(side).wait_send()
        for t in range(tiles):
            for j in range(nd):
                forward(side, j, t).wait_send()
            for h in range(halves):
                trade(t, side, h).wait_send()

    at_sides(sent)


def shards(
    nd, ns,
    initial_warmth, substance_label, neighbour_kernel, arriving_heat_rate, implicit_inverse_operator,
):
    layers_here, rows, width = initial_warmth.shape
    layers = implicit_inverse_operator.shape[0]
    tiles = width // nd // LANES
    halves = layers // LANES
    labels = substance_label[None, :]
    f32, dma = jnp.float32, pltpu.SemaphoreType.DMA

    def state(high):
        return pltpu.VMEM((tiles, halves, high, SPAN, LANES), f32)

    return settled(pl.pallas_call(
        functools.partial(kernel, nd, ns, tiles),
        out_shape=jax.ShapeDtypeStruct(initial_warmth.shape, f32),
        in_specs=[pl.BlockSpec(memory_space=pltpu.HBM)] * 5,
        out_specs=pl.BlockSpec(memory_space=pl.ANY),
        scratch_shapes=[
            pltpu.VMEM(labels.shape, labels.dtype),
            pltpu.SMEM(neighbour_kernel.shape, f32),
            pltpu.VMEM(arriving_heat_rate.shape, f32),
            pltpu.VMEM((layers, layers), f32),
            pltpu.VMEM((rows, layers_here, width), f32),
            pltpu.VMEM((tiles, rows, layers, LANES), f32),
            pltpu.VMEM((tiles, 2, rows, layers, LANES), f32),
            pltpu.VMEM((nd, layers_here, LANES), f32),
            pltpu.VMEM((layers, LANES), f32),
            pltpu.VMEM((halves, LANES, LANES), f32),
            pltpu.VMEM((2, halves, LANES, LANES), f32),
            pltpu.VMEM((2, rows, width), f32),
            state(rows + 8), state(rows + 4), state(rows + 4),
            pltpu.VMEM((rows + 4, (tiles + 2) * LANES, LANES), f32),
            pltpu.VMEM(((rows + 4) // 4, 8, SPAN, LANES), f32),
            pltpu.VMEM((rows + 4, WIDE, 2 * layers), jnp.bfloat16),
            pltpu.VMEM((tiles, rows, layers, LANES), f32),
            pltpu.VMEM((halves, 40, 8, LANES), f32),
            pltpu.VMEM((layers, 3 * layers), jnp.bfloat16),
            pltpu.VMEM((3 * layers, layers), jnp.bfloat16),
            dma((4,)), dma((rows,)),
            dma((nd, tiles + 1)), dma((nd, tiles + 1)), dma((tiles + 1,)),
            dma((2, nd, tiles)), dma((2, nd, tiles)), dma((2,)), dma((2,)), dma((2,)), dma((2,)),
            dma((tiles, 2, halves)), dma((tiles, 2, halves)),
            dma((nd, tiles, rows)), dma((nd, tiles, rows)), dma((tiles, rows)),
        ],
        compiler_params=pltpu.CompilerParams(
            collective_id=0, has_side_effects=True, vmem_limit_bytes=60 * 1024 * 1024
        ),
    )(initial_warmth, labels, neighbour_kernel, arriving_heat_rate, implicit_inverse_operator))


def settle(src_ref, out_ref, buf, i_sem, o_sem):
    pieces = i_sem.shape[0]
    each = src_ref.shape[0] // pieces

    def copy(k, out):
        part = pl.ds(k * each, each)
        if out:
            return pltpu.make_async_copy(buf.at[part], out_ref.at[part], o_sem.at[k])
        return pltpu.make_async_copy(src_ref.at[part], buf.at[part], i_sem.at[k])

    for k in range(pieces):
        copy(k, False).start()
    for k in range(pieces):
        copy(k, False).wait()
        copy(k, True).start()
    for k in range(pieces):
        copy(k, True).wait()


def settled(x):
    pieces = 8
    hbm = pl.BlockSpec(memory_space=pltpu.HBM)
    return pl.pallas_call(
        settle,
        out_shape=jax.ShapeDtypeStruct(x.shape, x.dtype),
        in_specs=[hbm],
        out_specs=hbm,
        scratch_shapes=[
            pltpu.VMEM(x.shape, x.dtype),
            pltpu.SemaphoreType.DMA((pieces,)), pltpu.SemaphoreType.DMA((pieces,)),
        ],
        compiler_params=pltpu.CompilerParams(vmem_limit_bytes=60 * 1024 * 1024),
    )(x)


def solution(mesh):
    return jax.shard_map(
        functools.partial(shards, mesh.shape["depth"], mesh.shape["surf"]),
        mesh=mesh,
        in_specs=(P("depth", "surf", None), P(), P(), P("surf", None), P()),
        out_specs=P("depth", "surf", None),
        check_vma=False,
    )
```
